128 devices in a mesh: dir: 4 (over z_hi, core), space: 32 (over y, x, z_lo).
Axes of the slice: x: 4, y: 4, z: 4 (z_hi: 2, z_lo: 2; z = z_hi * 2 + z_lo), core: 2. Of those that a mesh axis runs over, the one named last changes fastest.
Arguments:
- store: float32 [4, 2, 128, 512, 128], P('dir', None, 'space'), may hold values from 0.2 to 1.5
- rate: float32 [128, 512, 128], P('space'), may hold values from 0.3 to 3
- directions: float32 [8, 32, 8192], P('dir', 'space'), may hold values from -6 to 6
- owner_map: int32 [4], replicated, may hold values from 0 to 3, each once
- block_map: int32 [32], replicated, may hold values from 0 to 31, each once
Outputs:
- tangent: float32 [8, 2, 128, 512, 128], P('dir', None, 'space')
- sens: float32 [8, 32, 8192], P('dir', 'space')
The draws below stay inside these ranges and needn't reach their ends.
All inputs are finite; a program needn't handle non-finite values.
Results may differ from the reference program's by a relative error of at most 0.000071.
Values sent between devices are 32-bit elements; how exact they have to be, the bound alone decides.
A program may use at most 192 MiB of HBM per device.

```python
import math
import jax
import jax.numpy as jnp
from jax import lax

NY = 512
NZ = 128
STEPS = 2
SUBSTEPS = 3
DIRS = 8
NX = 128
CBLOCK = 8192
N_DIR = 4
N_SPACE = 32


def steps_of(rng, extent, split, least, high):
    loudness, own = 1.0, jax.random.fold_in(rng, 6)
    for axis_at, shards_of in split:
        heights = jnp.exp(jax.random.uniform(jax.random.fold_in(own, axis_at), (shards_of,), jnp.float32, least / len(split), high / len(split)))
        loudness = loudness * jnp.repeat(heights, extent[axis_at] // shards_of).reshape([-1 if axis == axis_at else 1 for axis in range(len(extent))])
    return loudness


def gaussian(key, dims, deviation, bound, shards=(), dtype=jnp.bfloat16):
    gain = steps_of(key, dims, shards, -0.22, 0.18) if shards else 1.0
    drawn = jax.random.normal(key, dims, jnp.float32) * deviation * gain
    return jnp.minimum(jnp.maximum(drawn, -bound), bound).astype(dtype)


def setup_inputs(seed: int = 0) -> dict:
    streams_of = jax.random.split(jax.random.key(seed), 6)
    store = jnp.clip(0.2 + 1.3 * jax.random.uniform(streams_of[0], (N_DIR, 2, NX, NY, NZ), jnp.float32) ** steps_of(streams_of[0], (N_DIR, 2, NX, NY, NZ), ((0, 4), (2, 32)), -0.2, 0.2), 0.2, 1.5)
    rate = jnp.clip(jnp.exp(math.log(3.0) - 2.3025851 * jax.random.uniform(streams_of[1], (NX, NY, NZ), jnp.float32) ** steps_of(streams_of[1], (NX, NY, NZ), ((0, 32),), -0.2, 0.2)), 0.3, 3.0)
    directions = gaussian(streams_of[2], (DIRS, N_SPACE, CBLOCK), 1.0, 6.0, ((0, 4), (1, 32)), jnp.float32)
    owner_map = jax.random.permutation(streams_of[3], N_DIR).astype(jnp.int32)
    block_map = jax.random.permutation(streams_of[4], N_SPACE).astype(jnp.int32)
    return {"store": store, "rate": rate, "directions": directions, "owner_map": owner_map, "block_map": block_map}


spread_a = 0.08
spread_b = 0.06
drift = 0.25
decay_rate = 0.05
rate_scale = 0.1


def advance(ext, slab, rate, vfine):
    centre = ext[:, 1:-1]
    padded = jnp.pad(centre, ((0, 0), (0, 0), (1, 1), (1, 1)))
    beside = ext[:, 2:] + ext[:, :-2]
    beside = beside + padded[:, :, 2:, 1:-1] + padded[:, :, :-2, 1:-1]
    beside = beside + padded[:, :, 1:-1, 2:] + padded[:, :, 1:-1, :-2]
    laplace = beside - 6.0 * centre
    upwind = centre - ext[:, :-2]
    first, second = centre[0], centre[1]
    conc_a, conc_b = slab[0], slab[1]
    source = rate_scale * rate * (vfine * conc_a * conc_b + first * conc_b + conc_a * second)
    first_new = first + spread_a * laplace[0] - drift * upwind[0] - source
    second_new = second + spread_b * laplace[1] - drift * upwind[1] + source - decay_rate * second
    return jnp.stack([first_new, second_new], 0)


def reference(store, rate, directions, owner_map, block_map):
    chosen = directions[:, block_map]
    coarse = chosen.reshape(DIRS, NX // 2, NY // 4, NZ // 4)

    def one_direction(coarse_one):
        vfine = jnp.repeat(jnp.repeat(jnp.repeat(coarse_one, 2, 0), 4, 1), 4, 2)
        state = jnp.zeros((2, NX, NY, NZ), jnp.float32)
        for step in range(STEPS):
            slab = lax.dynamic_index_in_dim(store, owner_map[step].astype(jnp.int32), 0, keepdims=False)
            for inner in range(SUBSTEPS):
                ext = jnp.pad(state, ((0, 0), (1, 1), (0, 0), (0, 0)))
                state = advance(ext, slab, rate, vfine)
        return state

    tangent = lax.map(one_direction, coarse)
    means = tangent[:, 1].reshape(DIRS, NX // 2, 2, NY // 4, 4, NZ // 4, 4).mean(axis=(2, 4, 6))
    coarse_q = means.reshape(DIRS, N_SPACE, CBLOCK)
    sens = jnp.zeros_like(coarse_q).at[:, block_map].set(coarse_q)
    return (tangent, sens)
```

```python
import jax
import jax.numpy as jnp
from jax import lax
from jax.experimental import pallas as pl
from jax.experimental.pallas import tpu as pltpu
from jax.sharding import PartitionSpec as P

N_SPACE = 32
NX = 128
ROWS = 264
PADR = 280
RC = 24
ORDER = (0, 3, 1, 2)
HI = lax.Precision.HIGHEST
F32 = jnp.float32


def remote(src, dst, send, recv, device):
    return pltpu.make_async_remote_copy(
        src_ref=src,
        dst_ref=dst,
        send_sem=send,
        recv_sem=recv,
        device_id=device,
        device_id_type=pl.DeviceIdType.MESH,
    )


def iota(shape, dim):
    return lax.broadcasted_iota(jnp.int32, shape, dim)


def sweep(
    owner, block, store, rate, dirs, out, sens,
    slab, cand0, cand1, ring0, ring1, ext0, ext1, rext, coef, vfine, state,
    got1, put2, got2, coarse, wide, umat, inverse, means, got3, put3,
    lsem, slab_s, slab_r, rz_s, rz_r, rx_s, rx_r,
    z0_s, z0_r, f0_s, f0_r, x0_s, x0_r, g_s, g_r,
    z1_s, z1_r, f1_s, f1_r, x1_s, x1_r,
    d1_s, d1_r, d2_s, d2_r, d3_s, d3_r, n1_s, n1_r, n1_x, n2_s, n2_r, o_s, o_r, o_l,
):
    me = lax.axis_index("space")
    di = lax.axis_index("dir")
    core = di % 2
    zh = di // 2
    zl = me % 2
    col = me // 2
    z = zh * 2 + zl
    up = (z + 1) % 4
    down = (z + 3) % 4
    zp = ((up // 2) * 2 + core, col * 2 + up % 2)
    zm = ((down // 2) * 2 + core, col * 2 + down % 2)
    mate = (zh * 2 + 1 - core, me)
    xr = (di, ((col + 1) % 16) * 2 + zl)
    xl = (di, ((col + 15) % 16) * 2 + zl)
    xt = (di, ((col + 1 + 14 * zl) % 16) * 2 + zl)
    near = 9 - 8 * zl
    far = 1 + 8 * zl
    own0 = jnp.where(owner[0] // 2 == zh, 1, 0)
    own1 = jnp.where(owner[1] // 2 == zh, 1, 0)
    core0 = owner[0] % 2
    core1 = owner[1] % 2

    barrier = pltpu.get_barrier_semaphore()

    @pl.loop(1, N_SPACE)
    def _(r):
        pl.semaphore_signal(
            barrier, inc=1, device_id=(di, (me + r) % N_SPACE), device_id_type=pl.DeviceIdType.MESH
        )

    @pl.loop(0, N_SPACE)
    def _(r):
        pl.semaphore_signal(
            barrier,
            inc=1,
            device_id=(zh * 2 + 1 - core, (me + r) % N_SPACE),
            device_id_type=pl.DeviceIdType.MESH,
        )

    other = ((1 - zh) * 2 + core, col * 2 + 1 - zl)
    pl.semaphore_signal(barrier, inc=1, device_id=other, device_id_type=pl.DeviceIdType.MESH)

    mine = pl.ds(248 * core, ROWS)
    theirs = pl.ds(248 * (1 - core), ROWS)
    local_slab = pltpu.make_async_copy(store.at[0, :, :, mine], slab.at[core], lsem.at[0])
    local_rate = pltpu.make_async_copy(rate.at[:, mine], rext.at[0], lsem.at[1])
    local_slab.start()
    local_rate.start()
    pl.semaphore_wait(barrier, 64)

    slab_copy = remote(store.at[0, :, :, theirs], slab.at[core], slab_s, slab_r, mate)
    slab_copy.start()

    @pl.loop(1, N_SPACE)
    def _(r):
        to = (me + r) % N_SPACE
        remote(dirs.at[:, to], got1.at[me], d1_s, d1_r, (di, to)).start()

    d1_local = pltpu.make_async_copy(dirs.at[:, me], got1.at[me], lsem.at[2])
    d1_local.start()

    rate_up = remote(rate.at[pl.ds(0, 2), mine], rext.at[1, pl.ds(0, 2)], rz_s.at[0], rz_r.at[0], zp)
    rate_down = remote(rate.at[pl.ds(2, 2), mine], rext.at[1, pl.ds(2, 2)], rz_s.at[1], rz_r.at[1], zm)
    rate_up.start()
    rate_down.start()

    @pl.loop(0, 14)
    def _(i):
        for d in range(4):
            for sp in range(2):
                for b in range(2):
                    state[b, d, sp, i] = jnp.zeros((PADR, 128), F32)

    local_slab.wait()
    slab_copy.wait_recv()

    def choose(cand, which):
        @pl.loop(0, 4)
        def _(i):
            for sp in range(2):
                first = jnp.broadcast_to(which == 0, (ROWS, 128))
                cand[sp, i] = jnp.where(first, slab[0, sp, i], slab[1, sp, i])

    def ring_copies(cand, ring, s, r):
        copies = []
        for i in ORDER:
            copies.append(remote(cand.at[:, i], ring.at[0, :, i], s.at[0, i], r.at[0, i], zp))
            copies.append(remote(cand.at[:, i], ring.at[1, :, i], s.at[1, i], r.at[1, i], zm))
        return copies

    choose(cand0, core0)
    ring_a = ring_copies(cand0, ring0, z0_s, z0_r)
    for copy in ring_a:
        copy.start()
    choose(cand1, core1)

    d1_local.wait()
    piece31 = got1.at[pl.ds(0, N_SPACE - 1)]
    remote(piece31, piece31, d1_s, d1_r, mate).wait_recv()
    late = jnp.where(me >= 16, 1, 0)

    @pl.loop(0, N_SPACE)
    def _(r):
        to = (me + r) % N_SPACE
        for e in range(4):
            at = jnp.clip(to + (e - 1) - late, 0, N_SPACE - 1)
            put2[r, e] = got1[block[at]]

    @pl.loop(1, N_SPACE)
    def _(r):
        to = (me + r) % N_SPACE
        remote(put2.at[r], got2.at[me], d2_s, d2_r, (di, to)).start()

    d2_local = pltpu.make_async_copy(put2.at[0], got2.at[me], lsem.at[3])
    d2_local.start()

    rate_x = []
    for h, copy in enumerate((rate_up, rate_down)):
        copy.wait_recv()
        part = pl.ds(2 * h, 2)
        rate_x.append(remote(rext.at[1, part], rext.at[2, part], rx_s.at[h], rx_r.at[h], xt))
        rate_x[-1].start()

    def ring_step(t, cand, ring, own, ext, z_r, f_s, f_r):
        forwards = []
        same = jnp.where(zl == 0, own, 1 - own)
        for i in ORDER:
            remote(cand.at[:, i], ring.at[0, :, i], f_s.at[i], z_r.at[0, i], zp).wait_recv()
            remote(cand.at[:, i], ring.at[1, :, i], f_s.at[i], z_r.at[1, i], zm).wait_recv()
            src, to = (0, zp) if i < 2 else (1, zm)
            copy = remote(ring.at[src, :, i], ring.at[2, :, i], f_s.at[i], f_r.at[i], to)
            copy.start()
            forwards.append(copy)
            for sp in range(2):
                from_up = jnp.broadcast_to(same == 1, (ROWS, 128))
                ext[0, sp, i] = jnp.where(from_up, ring[1, sp, i], ring[0, sp, i])
            if t == 0:
                copy = remote(ext.at[0, :, i], ext.at[1, :, i], x0_s.at[i], x0_r.at[i], xt)
                copy.start()
                forwards.append(copy)
        return forwards

    sent_a = ring_step(0, cand0, ring0, own0, ext0, z0_r, f0_s, f0_r)
    ring_b = ring_copies(cand1, ring1, z1_s, z1_r)
    for copy in ring_b:
        copy.start()

    @pl.loop(0, N_SPACE)
    def _(b):
        at = jnp.int32(0)
        for s in range(N_SPACE):
            at = jnp.where(block[s] == b, s, at)
        inverse[b] = at

    row = iota((ROWS, 128), 0) + 248 * core
    lane = iota((ROWS, 128), 1)
    cy = row >> 2
    umat[...] = jnp.where(((cy & 3) == (lane >> 5)) & ((cy >> 2) == (lane & 31)), 1.0, 0.0)

    d2_local.wait()
    piece31 = got2.at[pl.ds(0, N_SPACE - 1)]
    remote(piece31, piece31, d2_s, d2_r, mate).wait_recv()

    @pl.loop(0, 2)
    def _(d):
        for k in range(8):
            for jj in range(16):
                coarse[2 * core + d, k, 2 * jj : 2 * jj + 2] = got2[16 * (1 - k % 2) + jj, k // 2, d]

    coarse_mine = coarse.at[pl.ds(2 * core, 2)]
    coarse_copy = remote(coarse_mine, coarse_mine, d3_s, d3_r, mate)
    coarse_copy.start()
    coarse_copy.wait_recv()

    k_in = iota((128, 128), 0)
    k_out = iota((128, 128), 1)

    @pl.loop(0, 32)
    def _(n):
        d = n // 8
        k = n % 8
        block_c = coarse[d, k]
        for jj in range(4):
            w = jnp.where(k_in == 32 * jj + (k_out >> 2), 1.0, 0.0).astype(F32)
            wide[32 * jj : 32 * jj + 32] = jnp.dot(block_c, w, precision=HI, preferred_element_type=F32)
        vfine[d, k] = jnp.dot(umat[...], wide[...], precision=HI, preferred_element_type=F32)

    def put_coef(at, a, b, r):
        ra = 0.1 * r * a
        coef[0, at] = ra
        coef[1, at] = 0.1 * r * b
        coef[2, at] = ra * b

    def own_coef(cand, ring, own, i):
        here = jnp.broadcast_to(own == 1, (ROWS, 128))
        a = jnp.where(here, cand[0, i], ring[2, 0, i])
        b = jnp.where(here, cand[1, i], ring[2, 1, i])
        put_coef(5 + i, a, b, rext[0, i])

    local_rate.wait()
    for i in ORDER:
        remote(cand0.at[:, i], ring0.at[2, :, i], f0_s.at[i], f0_r.at[i], zp).wait_recv()
        own_coef(cand0, ring0, own0, i)
    edge_r = remote(coef.at[2, 8], coef.at[2, 0], g_s.at[0], g_r.at[0], xr)
    edge_l = remote(coef.at[2, 5], coef.at[2, 13], g_s.at[1], g_r.at[1], xl)
    edge_r.start()
    edge_l.start()

    @pl.loop(0, 4)
    def _(i):
        put_coef(near + i, ext0[0, 0, i], ext0[0, 1, i], rext[1, i])

    for copy in rate_x:
        copy.wait_recv()
    for i in ORDER:
        remote(ext0.at[0, :, i], ext0.at[1, :, i], x0_s.at[i], x0_r.at[i], xt).wait_recv()
        put_coef(far + i, ext0[1, 0, i], ext0[1, 1, i], rext[2, i])
    edge_r.wait_recv()
    edge_l.wait_recv()

    low = 5 - 4 * me
    high = NX + 5 - 4 * me

    @pl.loop(jnp.maximum(0, low), jnp.minimum(14, high))
    def _(i):
        k = (i + 1) // 2
        for d in range(4):
            src = vfine[d, k] * coef[2, i]
            state[0, d, 0, i, 8 : 8 + ROWS] = -src
            state[0, d, 1, i, 8 : 8 + ROWS] = src

    lanes = iota((RC, 128), 1)
    first_lane = lanes == 0
    last_lane = lanes == 127

    def plane(b, i):
        k = (i + 1) // 2

        @pl.loop(0, ROWS // RC)
        def _(n):
            at = pl.multiple_of(n * RC, 8)
            rows = pl.ds(at, RC)
            ra = coef[0, i, rows]
            rb = coef[1, i, rows]
            g = coef[2, i, rows]
            for d in range(4):
                def around(sp):
                    x = state[b, d, sp, i, pl.ds(at + 8, RC)]
                    low_x = state[b, d, sp, i - 1, pl.ds(at + 8, RC)]
                    s = state[b, d, sp, i + 1, pl.ds(at + 8, RC)]
                    s = s + state[b, d, sp, i, pl.ds(at + 7, RC)]
                    s = s + state[b, d, sp, i, pl.ds(at + 9, RC)]
                    s = s + jnp.where(first_lane, 0.0, pltpu.roll(x, 1, 1))
                    s = s + jnp.where(last_lane, 0.0, pltpu.roll(x, 127, 1))
                    return x, low_x, s

                p, p_low, p_sum = around(0)
                q, q_low, q_sum = around(1)
                src = vfine[d, k, rows] * g + p * rb + q * ra
                state[1 - b, d, 0, i, pl.ds(at + 8, RC)] = (
                    0.27 * p + 0.08 * p_sum + 0.33 * p_low - src
                )
                state[1 - b, d, 1, i, pl.ds(at + 8, RC)] = (
                    0.34 * q + 0.06 * q_sum + 0.31 * q_low + src
                )

    def update(u):
        @pl.loop(jnp.maximum(u - 1, low), jnp.minimum(15 - u, high))
        def _(i):
            plane(u % 2, i)

    update(2)
    update(3)

    sent_b = ring_step(1, cand1, ring1, own1, ext1, z1_r, f1_s, f1_r)
    part = pl.ds(2 - 2 * zl, 2)
    x1 = remote(ext1.at[0, :, part], ext1.at[1, :, part], x1_s, x1_r, xt)
    x1.start()
    edge_r.wait_send()
    edge_l.wait_send()
    for i in ORDER:
        remote(cand1.at[:, i], ring1.at[2, :, i], f1_s.at[i], f1_r.at[i], zp).wait_recv()
        own_coef(cand1, ring1, own1, i)
    x1.wait_recv()

    @pl.loop(0, 2)
    def _(i):
        n = i + 2 * zl
        put_coef(near + n, ext1[0, 0, n], ext1[0, 1, n], rext[1, n])
        m = i + 2 - 2 * zl
        put_coef(far + m, ext1[1, 0, m], ext1[1, 1, m], rext[2, m])

    update(4)
    update(5)

    half = pl.ds(256 * core, 256)
    held = pl.ds(8 + 8 * core, 256)

    def out_copies(i):
        here = pltpu.make_async_copy(
            state.at[1, pl.ds(2 * core, 2), :, 5 + i, held],
            out.at[:, :, i, half],
            o_l.at[i],
        )
        there = remote(
            state.at[1, pl.ds(2 - 2 * core, 2), :, 5 + i, held],
            out.at[:, :, i, half],
            o_s.at[i],
            o_r.at[i],
            mate,
        )
        return here, there

    srow = iota((64, 256), 0)
    scol = iota((64, 256), 1) >> 2

    @pl.loop(0, 4)
    def _(i):
        plane(0, 5 + i)
        here, there = out_copies(i)
        here.start()
        there.start()

    smat = jnp.where(scol == 4 * (srow & 15) + (srow >> 4), 1.0 / 32.0, 0.0).astype(F32)

    @pl.loop(0, 8)
    def _(n):
        cp = n // 4
        d = n % 4
        q = state[1, d, 1, 5 + 2 * cp, held] + state[1, d, 1, 6 + 2 * cp, held]
        m = jnp.dot(smat, q, precision=HI, preferred_element_type=F32)
        acc = jnp.zeros((16, 128), F32)
        for jj in range(4):
            t = jnp.where(k_out == 32 * jj + (k_in >> 2), 1.0, 0.0).astype(F32)
            acc = acc + jnp.dot(m[16 * jj : 16 * jj + 16], t, precision=HI, preferred_element_type=F32)
        for g in range(4):
            means[d // 2, (d % 2) * 8 + cp * 4 + g] = acc[4 * g : 4 * g + 4]

    self_piece = me // 16 == core

    @pl.loop(1, 16)
    def _(r):
        j = (me + r) % 16
        remote(means.at[core, j], got3.at[me], n1_s, n1_r, (di, 16 * core + j)).start()

    @pl.loop(0, 16)
    def _(r):
        j = (me + r) % 16
        remote(
            means.at[1 - core, j], got3.at[me], n1_s, n1_r, (zh * 2 + 1 - core, 16 * core + j)
        ).start()

    j0 = me % 16
    to_self = pltpu.make_async_copy(means.at[core, j0], got3.at[me], n1_r)
    to_twin = remote(means.at[core, j0], got3.at[me], n1_x, n1_r, (di, 16 * core + j0))

    @pl.when(self_piece)
    def _():
        to_self.start()

    @pl.when(jnp.logical_not(self_piece))
    def _():
        to_twin.start()

    remote(got3, got3, n1_s, n1_r, mate).wait_recv()

    @pl.loop(0, N_SPACE)
    def _(r):
        put3[r] = got3[inverse[(me + r) % N_SPACE]]

    cc = me // 16
    dl = (me // 8) % 2
    cp = (me // 4) % 2
    rg = me % 4

    @pl.loop(1, N_SPACE)
    def _(r):
        to = (me + r) % N_SPACE
        remote(put3.at[r], sens.at[dl, cp, cc, rg], n2_s, n2_r, (di, to)).start()

    sens_local = pltpu.make_async_copy(put3.at[0], sens.at[dl, cp, cc, rg], lsem.at[4])
    sens_local.start()

    sens_local.wait()
    piece31 = put3.at[pl.ds(0, N_SPACE - 1)]
    last = remote(piece31, piece31, n2_s, n2_r, mate)
    last.wait_send()
    last.wait_recv()
    remote(piece31, piece31, n1_s, n1_r, mate).wait_send()

    @pl.when(jnp.logical_not(self_piece))
    def _():
        to_twin.wait_send()

    for i in range(4):
        here, there = out_copies(i)
        here.wait()
        there.wait_send()
        there.wait_recv()
    piece31 = got1.at[pl.ds(0, N_SPACE - 1)]
    remote(piece31, piece31, d1_s, d1_r, mate).wait_send()
    piece31 = got2.at[pl.ds(0, N_SPACE - 1)]
    remote(piece31, piece31, d2_s, d2_r, mate).wait_send()
    coarse_copy.wait_send()
    slab_copy.wait_send()
    for copy in [rate_up, rate_down, x1] + rate_x + ring_a + ring_b + sent_a + sent_b:
        copy.wait_send()


def local(store, rate, directions, owner_map, block_map):
    dma = pltpu.SemaphoreType.DMA
    plane_pair = (2, 4, ROWS, 128)
    vmem = pltpu.VMEM
    scratch = [
        vmem((2,) + plane_pair, F32),
        vmem(plane_pair, F32),
        vmem(plane_pair, F32),
        vmem((3,) + plane_pair, F32),
        vmem((3,) + plane_pair, F32),
        vmem((2,) + plane_pair, F32),
        vmem((2,) + plane_pair, F32),
        vmem((3, 4, ROWS, 128), F32),
        vmem((3, 14, ROWS, 128), F32),
        vmem((4, 8, ROWS, 128), F32),
        vmem((2, 4, 2, 14, PADR, 128), F32),
        vmem((32, 2, 2, 128), F32),
        vmem((32, 4, 2, 2, 128), F32),
        vmem((32, 4, 2, 2, 128), F32),
        vmem((4, 8, 32, 128), F32),
        vmem((128, 128), F32),
        vmem((ROWS, 128), F32),
        pltpu.SMEM((32,), jnp.int32),
        vmem((2, 16, 4, 128), F32),
        vmem((32, 4, 128), F32),
        vmem((32, 4, 128), F32),
        dma((5,)), dma, dma, dma((2,)), dma((2,)), dma((2,)), dma((2,)),
        dma((2, 4)), dma((2, 4)), dma((4,)), dma((4,)), dma((4,)), dma((4,)), dma((2,)), dma((2,)),
        dma((2, 4)), dma((2, 4)), dma((4,)), dma((4,)), dma, dma,
        dma, dma, dma, dma, dma, dma, dma, dma, dma, dma, dma, dma((4,)), dma((4,)), dma((4,)),
    ]
    hbm = pl.BlockSpec(memory_space=pl.ANY)
    smem = pl.BlockSpec(memory_space=pltpu.SMEM)
    tangent, sens = pl.pallas_call(
        sweep,
        out_shape=(
            jax.ShapeDtypeStruct((2, 2, 4, 512, 128), F32),
            jax.ShapeDtypeStruct((2, 2, 2, 4, 4, 128), F32),
        ),
        in_specs=[smem, smem, hbm, hbm, hbm],
        out_specs=(hbm, hbm),
        scratch_shapes=scratch,
        compiler_params=pltpu.CompilerParams(
            collective_id=0, has_side_effects=True, vmem_limit_bytes=67043328
        ),
        name="sweep",
    )(owner_map, block_map, store, rate, directions.reshape(2, 32, 2, 128))
    return tangent, sens.reshape(2, 1, 8192)


def solution(mesh):
    return jax.shard_map(
        local,
        mesh=mesh,
        in_specs=(
            P("dir", None, "space", None, None),
            P("space", None, None),
            P("dir", "space", None),
            P(),
            P(),
        ),
        out_specs=(P("dir", None, "space", None, None), P("dir", "space", None)),
        check_vma=False,
    )
```

```python
import jax
import jax.numpy as jnp
from jax import lax
from jax.experimental import pallas as pl
from jax.experimental.pallas import tpu as pltpu
from jax.sharding import PartitionSpec as P

N_SPACE = 32
NX = 128
ROWS = 264
PADR = 280
RC = 24
PARTS = 11
ORDER = (0, 3, 1, 2)
F32 = jnp.float32
BF16 = jnp.bfloat16


def remote(src, dst, send, recv, device):
    return pltpu.make_async_remote_copy(
        src_ref=src,
        dst_ref=dst,
        send_sem=send,
        recv_sem=recv,
        device_id=device,
        device_id_type=pl.DeviceIdType.MESH,
    )


def one_hot(where):
    return jnp.where(where, 1.0, 0.0).astype(BF16)


def thirds(x):
    a = x.astype(BF16)
    rest = x - a.astype(F32)
    b = rest.astype(BF16)
    return a, b, (rest - b.astype(F32)).astype(BF16)


def iota(shape, dim):
    return lax.broadcasted_iota(jnp.int32, shape, dim)


def sweep(
    owner, block, store, rate, dirs, out, sens,
    slab, cand0, cand1, ring0, ring1, ext0, ext1, rext, coef, vfine, state,
    got1, put2, got2, coarse, wide, umat, wmat, tmat, smat, inverse, means, got3, put3,
    lsem, slab_s, slab_r, rz_s, rz_r, rx_s, rx_r,
    z0_s, z0_r, f0_s, f0_r, x0_s, x0_r, g_s, g_r,
    z1_s, z1_r, f1_s, f1_r, x1_s, x1_r,
    d1_s, d1_r, d2_s, d2_r, d3_s, d3_r, n1_s, n1_r, n1_x, n2_s, n2_r, o_s, o_r, o_l,
):
    me = lax.axis_index("space")
    di = lax.axis_index("dir")
    core = di % 2
    zh = di // 2
    zl = me % 2
    col = me // 2
    z = zh * 2 + zl
    up = (z + 1) % 4
    down = (z + 3) % 4
    zp = ((up // 2) * 2 + core, col * 2 + up % 2)
    zm = ((down // 2) * 2 + core, col * 2 + down % 2)
    mate = (zh * 2 + 1 - core, me)
    xr = (di, ((col + 1) % 16) * 2 + zl)
    xl = (di, ((col + 15) % 16) * 2 + zl)
    xt = (di, ((col + 1 + 14 * zl) % 16) * 2 + zl)
    near = 9 - 8 * zl
    far = 1 + 8 * zl
    own0 = jnp.where(owner[0] // 2 == zh, 1, 0)
    own1 = jnp.where(owner[1] // 2 == zh, 1, 0)
    core0 = owner[0] % 2
    core1 = owner[1] % 2

    barrier = pltpu.get_barrier_semaphore()

    @pl.loop(1, N_SPACE)
    def _(r):
        pl.semaphore_signal(
            barrier, inc=1, device_id=(di, (me + r) % N_SPACE), device_id_type=pl.DeviceIdType.MESH
        )

    @pl.loop(0, N_SPACE)
    def _(r):
        pl.semaphore_signal(
            barrier,
            inc=1,
            device_id=(zh * 2 + 1 - core, (me + r) % N_SPACE),
            device_id_type=pl.DeviceIdType.MESH,
        )

    other = ((1 - zh) * 2 + core, col * 2 + 1 - zl)
    pl.semaphore_signal(barrier, inc=1, device_id=other, device_id_type=pl.DeviceIdType.MESH)

    mine = pl.ds(248 * core, ROWS)
    theirs = pl.ds(248 * (1 - core), ROWS)
    local_slab = pltpu.make_async_copy(store.at[0, :, :, mine], slab.at[core], lsem.at[0])
    local_rate = pltpu.make_async_copy(rate.at[:, mine], rext.at[0], lsem.at[1])
    local_slab.start()
    local_rate.start()
    @pl.loop(0, 14)
    def _(i):
        for d in range(4):
            for sp in range(2):
                for b in range(2):
                    state[b, d, sp, i] = jnp.zeros((PADR, 128), F32)

    pl.semaphore_wait(barrier, 64)

    slab_copy = remote(store.at[0, :, :, theirs], slab.at[core], slab_s, slab_r, mate)
    slab_copy.start()

    @pl.loop(1, N_SPACE)
    def _(r):
        to = (me + r) % N_SPACE
        remote(dirs.at[:, to], got1.at[me], d1_s, d1_r, (di, to)).start()

    d1_local = pltpu.make_async_copy(dirs.at[:, me], got1.at[me], lsem.at[2])
    d1_local.start()

    rate_up = remote(rate.at[pl.ds(0, 2), mine], rext.at[1, pl.ds(0, 2)], rz_s.at[0], rz_r.at[0], zp)
    rate_down = remote(rate.at[pl.ds(2, 2), mine], rext.at[1, pl.ds(2, 2)], rz_s.at[1], rz_r.at[1], zm)
    rate_up.start()
    rate_down.start()

    local_slab.wait()
    slab_copy.wait_recv()

    def choose(cand, which):
        @pl.loop(0, 4)
        def _(i):
            for sp in range(2):
                first = jnp.broadcast_to(which == 0, (ROWS, 128))
                cand[sp, i] = jnp.where(first, slab[0, sp, i], slab[1, sp, i])

    def ring_copies(cand, ring, s, r):
        copies = []
        for i in ORDER:
            copies.append(remote(cand.at[:, i], ring.at[0, :, i], s.at[0, i], r.at[0, i], zp))
            copies.append(remote(cand.at[:, i], ring.at[1, :, i], s.at[1, i], r.at[1, i], zm))
        return copies

    choose(cand0, core0)
    ring_a = ring_copies(cand0, ring0, z0_s, z0_r)
    for copy in ring_a[:2]:
        copy.start()
    choose(cand1, core1)

    d1_local.wait()
    piece31 = got1.at[pl.ds(0, N_SPACE - 1)]
    remote(piece31, piece31, d1_s, d1_r, mate).wait_recv()
    late = jnp.where(me >= 16, 1, 0)

    @pl.loop(0, N_SPACE)
    def _(r):
        to = (me + r) % N_SPACE
        for e in range(4):
            at = jnp.clip(to + (e - 1) - late, 0, N_SPACE - 1)
            put2[r, e] = got1[block[at]]

    @pl.loop(1, N_SPACE)
    def _(r):
        to = (me + r) % N_SPACE
        remote(put2.at[r], got2.at[me], d2_s, d2_r, (di, to)).start()

    d2_local = pltpu.make_async_copy(put2.at[0], got2.at[me], lsem.at[3])
    d2_local.start()

    for copy in ring_a[2:]:
        copy.start()

    rate_x = []
    for h, copy in enumerate((rate_up, rate_down)):
        copy.wait_recv()
        part = pl.ds(2 * h, 2)
        rate_x.append(remote(rext.at[1, part], rext.at[2, part], rx_s.at[h], rx_r.at[h], xt))
        rate_x[-1].start()

    def ring_step(t, cand, ring, own, ext, z_r, f_s, f_r, planes):
        forwards = []
        same = jnp.where(zl == 0, own, 1 - own)
        for i in planes:
            remote(cand.at[:, i], ring.at[0, :, i], f_s.at[i], z_r.at[0, i], zp).wait_recv()
            remote(cand.at[:, i], ring.at[1, :, i], f_s.at[i], z_r.at[1, i], zm).wait_recv()
            src, to = (0, zp) if i < 2 else (1, zm)
            copy = remote(ring.at[src, :, i], ring.at[2, :, i], f_s.at[i], f_r.at[i], to)
            copy.start()
            forwards.append(copy)
            for sp in range(2):
                from_up = jnp.broadcast_to(same == 1, (ROWS, 128))
                ext[0, sp, i] = jnp.where(from_up, ring[1, sp, i], ring[0, sp, i])
            if t == 0:
                copy = remote(ext.at[0, :, i], ext.at[1, :, i], x0_s.at[i], x0_r.at[i], xt)
                copy.start()
                forwards.append(copy)
        return forwards

    @pl.loop(0, N_SPACE)
    def _(b):
        at = jnp.int32(0)
        for s in range(N_SPACE):
            at = jnp.where(block[s] == b, s, at)
        inverse[b] = at

    row = iota((ROWS, 128), 0) + 248 * core
    lane = iota((ROWS, 128), 1)
    cy = row >> 2
    umat[...] = one_hot(((cy & 3) == (lane >> 5)) & ((cy >> 2) == (lane & 31)))
    k_in = iota((128, 128), 0)
    k_out = iota((128, 128), 1)
    for jj in range(4):
        wmat[:, 128 * jj : 128 * jj + 128] = one_hot(k_in == 32 * jj + (k_out >> 2))
        tmat[jj] = one_hot(k_out == 32 * jj + (k_in >> 2))
    srow = iota((64, 256), 0)
    scol = iota((64, 256), 1) >> 2
    smat[...] = one_hot(scol == 4 * (srow & 15) + (srow >> 4))

    args_a = (0, cand0, ring0, own0, ext0, z0_r, f0_s, f0_r)
    sent_a = ring_step(*args_a, ORDER[:2])

    d2_local.wait()
    piece31 = got2.at[pl.ds(0, N_SPACE - 1)]
    remote(piece31, piece31, d2_s, d2_r, mate).wait_recv()

    @pl.loop(0, 2)
    def _(d):
        for k in range(8):
            for jj in range(16):
                coarse[2 * core + d, k, 2 * jj : 2 * jj + 2] = got2[16 * (1 - k % 2) + jj, k // 2, d]

    coarse_mine = coarse.at[pl.ds(2 * core, 2)]
    coarse_copy = remote(coarse_mine, coarse_mine, d3_s, d3_r, mate)
    coarse_copy.start()

    sent_a += ring_step(*args_a, ORDER[2:3])
    coarse_copy.wait_recv()

    def expand(n):
        d = n // 8
        k = n % 8
        total = jnp.zeros((ROWS, 128), F32)
        for h, part in enumerate(thirds(coarse[d, k])):
            x = jnp.dot(part, wmat[...], preferred_element_type=F32).astype(BF16)
            for jj in range(4):
                wide[h, 32 * jj : 32 * jj + 32] = x[:, 128 * jj : 128 * jj + 128]
            total = total + jnp.dot(umat[...], wide[h], preferred_element_type=F32)
        vfine[d, k] = total

    pl.loop(0, 16)(expand)
    sent_a += ring_step(*args_a, ORDER[3:])
    ring_b = ring_copies(cand1, ring1, z1_s, z1_r)
    for copy in ring_b:
        copy.start()
    pl.loop(16, 32)(expand)

    def put_coef(at, a, b, r):
        ra = 0.1 * r * a
        coef[0, at] = ra
        coef[1, at] = 0.1 * r * b
        coef[2, at] = ra * b

    def own_coef(cand, ring, own, i):
        here = jnp.broadcast_to(own == 1, (ROWS, 128))
        a = jnp.where(here, cand[0, i], ring[2, 0, i])
        b = jnp.where(here, cand[1, i], ring[2, 1, i])
        put_coef(5 + i, a, b, rext[0, i])

    local_rate.wait()
    for i in ORDER:
        remote(cand0.at[:, i], ring0.at[2, :, i], f0_s.at[i], f0_r.at[i], zp).wait_recv()
        own_coef(cand0, ring0, own0, i)
    edge_r = remote(coef.at[2, 8], coef.at[2, 0], g_s.at[0], g_r.at[0], xr)
    edge_l = remote(coef.at[2, 5], coef.at[2, 13], g_s.at[1], g_r.at[1], xl)
    edge_r.start()
    edge_l.start()

    @pl.loop(0, 4)
    def _(i):
        put_coef(near + i, ext0[0, 0, i], ext0[0, 1, i], rext[1, i])

    for copy in rate_x:
        copy.wait_recv()
    for i in ORDER:
        remote(ext0.at[0, :, i], ext0.at[1, :, i], x0_s.at[i], x0_r.at[i], xt).wait_recv()
        put_coef(far + i, ext0[1, 0, i], ext0[1, 1, i], rext[2, i])
    edge_r.wait_recv()
    edge_l.wait_recv()

    low = 5 - 4 * me
    high = NX + 5 - 4 * me

    @pl.loop(jnp.maximum(0, low), jnp.minimum(14, high))
    def _(i):
        k = (i + 1) // 2
        for d in range(4):
            src = vfine[d, k] * coef[2, i]
            state[0, d, 0, i, 8 : 8 + ROWS] = -src
            state[0, d, 1, i, 8 : 8 + ROWS] = src

    lanes = iota((RC, 128), 1)
    first_lane = lanes == 0
    last_lane = lanes == 127

    def rows_of(b, i, k, at):
        rows = pl.ds(at, RC)
        ra = coef[0, i, rows]
        rb = coef[1, i, rows]
        g = coef[2, i, rows]
        for d in range(4):
            def around(sp):
                x = state[b, d, sp, i, pl.ds(at + 8, RC)]
                low_x = state[b, d, sp, i - 1, pl.ds(at + 8, RC)]
                s = state[b, d, sp, i + 1, pl.ds(at + 8, RC)]
                s = s + state[b, d, sp, i, pl.ds(at + 7, RC)]
                s = s + state[b, d, sp, i, pl.ds(at + 9, RC)]
                s = s + jnp.where(first_lane, 0.0, pltpu.roll(x, 1, 1))
                s = s + jnp.where(last_lane, 0.0, pltpu.roll(x, 127, 1))
                return x, low_x, s

            p, p_low, p_sum = around(0)
            q, q_low, q_sum = around(1)
            src = vfine[d, k, rows] * g + p * rb + q * ra
            state[1 - b, d, 0, i, pl.ds(at + 8, RC)] = (
                0.27 * p + 0.08 * p_sum + 0.33 * p_low - src
            )
            state[1 - b, d, 1, i, pl.ds(at + 8, RC)] = (
                0.34 * q + 0.06 * q_sum + 0.31 * q_low + src
            )

    def planes(b, start, stop):
        @pl.loop(start, stop)
        def _(i):
            k = (i + 1) // 2

            @pl.loop(0, ROWS // (RC * PARTS))
            def _(n):
                for h in range(PARTS):
                    rows_of(b, i, k, pl.multiple_of(n * (RC * PARTS) + h * RC, 8))

    def update(u):
        planes(u % 2, jnp.maximum(u - 1, low), jnp.minimum(15 - u, high))

    update(2)
    args_b = (1, cand1, ring1, own1, ext1, z1_r, f1_s, f1_r)
    sent_b = ring_step(*args_b, ORDER[:2])
    update(3)
    sent_b += ring_step(*args_b, ORDER[2:])
    part = pl.ds(2 - 2 * zl, 2)
    x1 = remote(ext1.at[0, :, part], ext1.at[1, :, part], x1_s, x1_r, xt)
    x1.start()
    edge_r.wait_send()
    edge_l.wait_send()
    for i in ORDER:
        remote(cand1.at[:, i], ring1.at[2, :, i], f1_s.at[i], f1_r.at[i], zp).wait_recv()
        own_coef(cand1, ring1, own1, i)
    x1.wait_recv()

    @pl.loop(0, 2)
    def _(i):
        n = i + 2 * zl
        put_coef(near + n, ext1[0, 0, n], ext1[0, 1, n], rext[1, n])
        m = i + 2 - 2 * zl
        put_coef(far + m, ext1[1, 0, m], ext1[1, 1, m], rext[2, m])

    update(4)
    update(5)

    half = pl.ds(256 * core, 256)
    held = pl.ds(8 + 8 * core, 256)

    def out_copies(i):
        here = pltpu.make_async_copy(
            state.at[1, pl.ds(2 * core, 2), :, 5 + i, held],
            out.at[:, :, i, half],
            o_l.at[i],
        )
        there = remote(
            state.at[1, pl.ds(2 - 2 * core, 2), :, 5 + i, held],
            out.at[:, :, i, half],
            o_s.at[i],
            o_r.at[i],
            mate,
        )
        return here, there

    @pl.loop(0, 4)
    def _(i):
        planes(0, 5 + i, 6 + i)
        here, there = out_copies(i)
        here.start()
        there.start()

    @pl.loop(0, 8)
    def _(n):
        cp = n // 4
        d = n % 4
        q = (state[1, d, 1, 5 + 2 * cp, held] + state[1, d, 1, 6 + 2 * cp, held]) * (1.0 / 32.0)
        m = jnp.zeros((64, 128), F32)
        for part in thirds(q):
            m = m + jnp.dot(smat[...], part, preferred_element_type=F32)
        acc = jnp.zeros((16, 128), F32)
        for part in thirds(m):
            for jj in range(4):
                acc = acc + jnp.dot(
                    part[16 * jj : 16 * jj + 16], tmat[jj], preferred_element_type=F32
                )
        for g in range(4):
            means[d // 2, (d % 2) * 8 + cp * 4 + g] = acc[4 * g : 4 * g + 4]

    self_piece = me // 16 == core

    @pl.loop(1, 16)
    def _(r):
        j = (me + r) % 16
        remote(means.at[core, j], got3.at[me], n1_s, n1_r, (di, 16 * core + j)).start()

    @pl.loop(0, 16)
    def _(r):
        j = (me + r) % 16
        remote(
            means.at[1 - core, j], got3.at[me], n1_s, n1_r, (zh * 2 + 1 - core, 16 * core + j)
        ).start()

    j0 = me % 16
    to_self = pltpu.make_async_copy(means.at[core, j0], got3.at[me], n1_r)
    to_twin = remote(means.at[core, j0], got3.at[me], n1_x, n1_r, (di, 16 * core + j0))

    @pl.when(self_piece)
    def _():
        to_self.start()

    @pl.when(jnp.logical_not(self_piece))
    def _():
        to_twin.start()

    remote(got3, got3, n1_s, n1_r, mate).wait_recv()

    @pl.loop(0, N_SPACE)
    def _(r):
        put3[r] = got3[inverse[(me + r) % N_SPACE]]

    cc = me // 16
    dl = (me // 8) % 2
    cp = (me // 4) % 2
    rg = me % 4

    @pl.loop(1, N_SPACE)
    def _(r):
        to = (me + r) % N_SPACE
        remote(put3.at[r], sens.at[dl, cp, cc, rg], n2_s, n2_r, (di, to)).start()

    sens_local = pltpu.make_async_copy(put3.at[0], sens.at[dl, cp, cc, rg], lsem.at[4])
    sens_local.start()

    sens_local.wait()
    piece31 = put3.at[pl.ds(0, N_SPACE - 1)]
    last = remote(piece31, piece31, n2_s, n2_r, mate)
    last.wait_send()
    last.wait_recv()
    remote(piece31, piece31, n1_s, n1_r, mate).wait_send()

    @pl.when(jnp.logical_not(self_piece))
    def _():
        to_twin.wait_send()

    for i in range(4):
        here, there = out_copies(i)
        here.wait()
        there.wait_send()
        there.wait_recv()
    piece31 = got1.at[pl.ds(0, N_SPACE - 1)]
    remote(piece31, piece31, d1_s, d1_r, mate).wait_send()
    piece31 = got2.at[pl.ds(0, N_SPACE - 1)]
    remote(piece31, piece31, d2_s, d2_r, mate).wait_send()
    coarse_copy.wait_send()
    slab_copy.wait_send()
    for copy in [rate_up, rate_down, x1] + rate_x + ring_a + ring_b + sent_a + sent_b:
        copy.wait_send()


def local(store, rate, directions, owner_map, block_map):
    dma = pltpu.SemaphoreType.DMA
    plane_pair = (2, 4, ROWS, 128)
    vmem = pltpu.VMEM
    scratch = [
        vmem((2,) + plane_pair, F32),
        vmem(plane_pair, F32),
        vmem(plane_pair, F32),
        vmem((3,) + plane_pair, F32),
        vmem((3,) + plane_pair, F32),
        vmem((2,) + plane_pair, F32),
        vmem((2,) + plane_pair, F32),
        vmem((3, 4, ROWS, 128), F32),
        vmem((3, 14, ROWS, 128), F32),
        vmem((4, 8, ROWS, 128), F32),
        vmem((2, 4, 2, 14, PADR, 128), F32),
        vmem((32, 2, 2, 128), F32),
        vmem((32, 4, 2, 2, 128), F32),
        vmem((32, 4, 2, 2, 128), F32),
        vmem((4, 8, 32, 128), F32),
        vmem((3, 128, 128), BF16),
        vmem((ROWS, 128), BF16),
        vmem((128, 512), BF16),
        vmem((4, 128, 128), BF16),
        vmem((64, 256), BF16),
        pltpu.SMEM((32,), jnp.int32),
        vmem((2, 16, 4, 128), F32),
        vmem((32, 4, 128), F32),
        vmem((32, 4, 128), F32),
        dma((5,)), dma, dma, dma((2,)), dma((2,)), dma((2,)), dma((2,)),
        dma((2, 4)), dma((2, 4)), dma((4,)), dma((4,)), dma((4,)), dma((4,)), dma((2,)), dma((2,)),
        dma((2, 4)), dma((2, 4)), dma((4,)), dma((4,)), dma, dma,
        dma, dma, dma, dma, dma, dma, dma, dma, dma, dma, dma, dma((4,)), dma((4,)), dma((4,)),
    ]
    hbm = pl.BlockSpec(memory_space=pl.ANY)
    smem = pl.BlockSpec(memory_space=pltpu.SMEM)
    tangent, sens = pl.pallas_call(
        sweep,
        out_shape=(
            jax.ShapeDtypeStruct((2, 2, 4, 512, 128), F32),
            jax.ShapeDtypeStruct((2, 2, 2, 4, 4, 128), F32),
        ),
        in_specs=[smem, smem, hbm, hbm, hbm],
        out_specs=(hbm, hbm),
        scratch_shapes=scratch,
        compiler_params=pltpu.CompilerParams(
            collective_id=0, has_side_effects=True, vmem_limit_bytes=67043328
        ),
        name="sweep",
    )(owner_map, block_map, store, rate, directions.reshape(2, 32, 2, 128))
    return tangent, sens.reshape(2, 1, 8192)


def solution(mesh):
    return jax.shard_map(
        local,
        mesh=mesh,
        in_specs=(
            P("dir", None, "space", None, None),
            P("space", None, None),
            P("dir", "space", None),
            P(),
            P(),
        ),
        out_specs=(P("dir", None, "space", None, None), P("dir", "space", None)),
        check_vma=False,
    )
```
